32 devices in a mesh: tower: 2 (over x), dp: 16 (over z, y, core).
Axes of the slice: x: 2, y: 2, z: 4, core: 2. Of those that a mesh axis runs over, the one named last changes fastest.
Arguments:
- images: bfloat16 [288, 50, 768], P('dp'), may hold values from -6 to 6
- captions: bfloat16 [864, 16, 768], P('dp'), may hold values from -6 to 6
- token_ids: int32 [864, 16], P('dp'), may hold values from 0 to 31999, as said below
- counts: int32 [288], P('dp'), may hold values from 1 to 5, as said below
- matches: int32 [864], P('dp'), may hold values from 0 to 287, as said below
- image_weights: bfloat16 [9216, 768], P('dp')
- image_norms: float32 [4, 768], replicated, may hold values from -1.2 to 1.2, as said below
- weights: float32 [9216, 768], P(('tower', 'dp'))
- norm_params: float32 [4, 768], replicated, may hold values from -1.2 to 1.2, as said below
- momentum: float32 [9216, 768], P(('tower', 'dp'))
- norm_momentum: float32 [4, 768], replicated
- averages: float32 [9216, 768], P(('tower', 'dp'))
- norm_averages: float32 [4, 768], replicated, may hold values from -1.2 to 1.2
Outputs:
- grads: float32 [9216, 768], P(('tower', 'dp'))
- norm_grads: float32 [4, 768], replicated
- input_grad: float32 [864, 16, 768], P('dp', None, 'tower')
- new_weights: float32 [9216, 768], P(('tower', 'dp'))
- new_momentum: float32 [9216, 768], P(('tower', 'dp'))
- new_averages: float32 [9216, 768], P(('tower', 'dp'))
- new_norm_params: float32 [4, 768], replicated
- new_norm_momentum: float32 [4, 768], replicated
- new_norm_averages: float32 [4, 768], replicated
- grad_norm: float32 [], replicated
The draws below stay inside these ranges and needn't reach their ends.
Inputs may be any that keep to these rules, and one draw needn't show every extreme that they name: `token_ids`: in each caption the ids are nonzero on a leading run of 4 to 16 positions and 0 after it. counts[i] is the number of captions c with matches[c] = i; the counts sum to 864. `matches`: image i is named by exactly counts[i] captions. `norm_params`: rows 0 and 2 are gains, rows 1 and 3 biases. `image_norms`: rows 0 and 2 are gains, rows 1 and 3 biases.
All inputs are finite; a program needn't handle non-finite values.
Results may differ from the reference program's by a relative error of at most 0.014.
The reference program's roundings to bfloat16 on the way count: a program that leaves them out, or rounds other values in their place, can miss the bound.
Values may be sent and summed in bfloat16 or wider, within the bound.
No kernel may reach another device: no remote copies, remote signals or barrier semaphores. Data moves between devices by JAX's collectives and lax.ppermute only.
A program may use at most 320 MiB of HBM per device.

```python
import math
import jax
import jax.numpy as jnp
from jax import lax

D = 768
HEADS = 12
HEAD_DIM = 64
FF = 3072
IMG_ROWS = 50
TXT_LEN = 16
VOCAB = 32000
IMG_DEV = 18
CAP_DEV = 54
IMAGES = 288
CAPTIONS = 864
WROWS = 9216
N_DP = 16


def pair_counts(key):
    base_key = jax.random.fold_in(key, 11)
    first_key, order_key, shuffle_key = jax.random.split(base_key, 3)
    halves = jax.random.randint(first_key, (IMAGES // 2,), 1, 6)
    halves = halves.at[0].set(5)
    placed = jnp.stack([halves, 6 - halves], axis=1).reshape(IMAGES)
    ordering = jax.random.permutation(order_key, IMAGES)
    counts = jnp.zeros((IMAGES,), jnp.int32).at[ordering].set(placed.astype(jnp.int32))
    return (counts, shuffle_key)


def draw_counts(key, part):
    return pair_counts(key)[0]


def draw_matches(key, part):
    counts, shuffle_key = pair_counts(key)
    listed = jnp.repeat(jnp.arange(IMAGES, dtype=jnp.int32), counts, total_repeat_length=CAPTIONS)
    return listed[jax.random.permutation(shuffle_key, CAPTIONS)]


def draw_token_ids(key, part):
    length_key, word_key = jax.random.split(jax.random.fold_in(key, 23))
    lengths = jax.random.randint(length_key, (CAPTIONS,), 4, TXT_LEN + 1)
    lengths = lengths.at[0].set(TXT_LEN).at[1].set(4)
    words = jax.random.randint(word_key, (CAPTIONS, TXT_LEN), 1, VOCAB)
    words = words.at[0, 0].set(VOCAB - 1)
    places = jnp.arange(TXT_LEN)[None, :]
    return jnp.where(places < lengths[:, None], words, 0).astype(jnp.int32)


def row_scales(attention_gain):
    rows_index = jnp.arange(WROWS)
    first = D ** (-0.5)
    return jnp.where(rows_index < 3 * D, first, jnp.where(rows_index < 4 * D, attention_gain * first, jnp.where(rows_index < 4 * D + FF, first, FF ** (-0.5))))


def matrix_draw(key, stream, attention_gain):
    sample_key = jax.random.fold_in(key, stream)
    sample = jnp.clip(jax.random.normal(sample_key, (WROWS, D), jnp.float32), -4.0, 4.0)
    return sample * row_scales(attention_gain)[:, None]


def draw_weights(key, part):
    return matrix_draw(key, 31, 2.5)


def draw_image_weights(key, part):
    return matrix_draw(key, 37, 4.0).astype(jnp.bfloat16)


def draw_averages(key, part):
    return matrix_draw(key, 41, 2.5)


def norm_rows(key, stream):
    gain_key, shift_key = jax.random.split(jax.random.fold_in(key, stream))
    gain_rows = 1.0 + 0.15 * jax.random.uniform(gain_key, (2, D), jnp.float32, -1.0, 1.0)
    shifts = 0.3 * jnp.clip(jax.random.normal(shift_key, (2, D), jnp.float32), -4.0, 4.0)
    return jnp.stack([gain_rows[0], shifts[0], gain_rows[1], shifts[1]])


def draw_image_norms(key, part):
    return norm_rows(key, 43)


def draw_norm_params(key, part):
    return norm_rows(key, 47)


def draw_norm_averages(key, part):
    return norm_rows(key, 53)


def draw_momentum(key, part):
    sample = jax.random.normal(jax.random.fold_in(key, 59), (WROWS, D), jnp.float32)
    return sample * (1.1 / math.sqrt(WROWS * D))


def draw_norm_momentum(key, part):
    sample = jax.random.normal(jax.random.fold_in(key, 61), (4, D), jnp.float32)
    return sample * (3.0 / math.sqrt(WROWS * D))


def level_of(key, dims, shards, smallest, largest):
    level, own = 1.0, jax.random.fold_in(key, 6)
    for dim, shards_of in shards:
        steps = jnp.exp(jax.random.uniform(jax.random.fold_in(own, dim), (shards_of,), jnp.float32, smallest / len(shards), largest / len(shards)))
        level = level * jnp.repeat(steps, dims[dim] // shards_of).reshape([-1 if axis == dim else 1 for axis in range(len(dims))])
    return level


def bell_draw(key, dims, deviation, most, shards=(), kind=jnp.bfloat16):
    factor_of = level_of(key, dims, shards, -0.22, 0.18) if shards else 1.0
    drawn = jax.random.normal(key, dims, jnp.float32) * deviation * factor_of
    return jnp.minimum(jnp.maximum(drawn, -most), most).astype(kind)


def setup_inputs(seed: int = 0) -> dict:
    keys = jax.random.split(jax.random.key(seed), 14)
    images = bell_draw(keys[0], (IMAGES, IMG_ROWS, D), 1.0, 6.0, ((0, 16),))
    captions = bell_draw(keys[1], (CAPTIONS, TXT_LEN, D), 1.0, 6.0, ((0, 16),))
    token_ids = draw_token_ids(jax.random.fold_in(keys[13], 71), 0)
    counts = draw_counts(jax.random.fold_in(keys[13], 71), 0)
    matches = draw_matches(jax.random.fold_in(keys[13], 71), 0)
    image_weights = draw_image_weights(jax.random.fold_in(keys[13], 71), 0)
    image_norms = draw_image_norms(jax.random.fold_in(keys[13], 71), 0)
    weights = draw_weights(jax.random.fold_in(keys[13], 71), 0)
    norm_params = draw_norm_params(jax.random.fold_in(keys[13], 71), 0)
    momentum = draw_momentum(jax.random.fold_in(keys[13], 71), 0)
    norm_momentum = draw_norm_momentum(jax.random.fold_in(keys[13], 71), 0)
    averages = draw_averages(jax.random.fold_in(keys[13], 71), 0)
    norm_averages = draw_norm_averages(jax.random.fold_in(keys[13], 71), 0)
    return {"images": images, "captions": captions, "token_ids": token_ids, "counts": counts, "matches": matches, "image_weights": image_weights, "image_norms": image_norms, "weights": weights, "norm_params": norm_params, "momentum": momentum, "norm_momentum": norm_momentum, "averages": averages, "norm_averages": norm_averages}


@jax.custom_vjp
def low(v):
    return lax.optimization_barrier(v.astype(jnp.bfloat16)).astype(jnp.float32)

@jax.custom_vjp
def low_back(v):
    return v

def low_keep(v):
    return (low(v), None)

def low_pass(kept, grad):
    return (grad,)

def back_keep(v):
    return (v, None)

def back_low(kept, grad):
    return (low(grad),)
low.defvjp(low_keep, low_pass)
low_back.defvjp(back_keep, back_low)
EPSILON = 1e-06
LOGIT_SCALE = 50.0
CLIP_NORM = 1.0
MOMENTUM_RATE = 0.9
DECAY_RATE = 0.0001
AVERAGE_RATE = 0.7

def layer_norm(rows_in, scaling, offset):
    middle = lax.optimization_barrier(jnp.mean(rows_in, axis=-1, keepdims=True))
    centred = rows_in - middle
    spread = lax.optimization_barrier(jnp.mean(centred * centred, axis=-1, keepdims=True))
    return centred * lax.rsqrt(spread + EPSILON) * scaling + offset

def product(left, right):
    return jnp.einsum('...k,nk->...n', left, right, precision=lax.Precision.HIGHEST)

def block_forward(rows_in, packed, norms, causal):
    features = rows_in.shape[-1]
    hidden_units = (packed.shape[0] - 4 * features) // 2
    qkv_matrix = packed[:3 * features]
    out_matrix = packed[3 * features:4 * features]
    up_matrix = packed[4 * features:4 * features + hidden_units]
    down_matrix = packed[4 * features + hidden_units:]
    seq_count, seq_length = (rows_in.shape[0], rows_in.shape[1])
    normed = low(layer_norm(rows_in, norms[0], norms[1]))
    joined = low(product(normed, qkv_matrix)).reshape(seq_count, seq_length, 3, HEADS, HEAD_DIM)
    queries = low_back(joined[:, :, 0])
    key_rows = low_back(joined[:, :, 1])
    values = low_back(joined[:, :, 2])
    scores = low_back(jnp.einsum('nqhd,nkhd->nhqk', queries, key_rows, precision=lax.Precision.HIGHEST)) * HEAD_DIM ** (-0.5)
    if causal:
        causal_mask = jnp.arange(seq_length)[:, None] >= jnp.arange(seq_length)[None, :]
        scores = jnp.where(causal_mask, scores, -1e+30)
    attn_probs = low(jax.nn.softmax(scores, axis=-1))
    attended = jnp.einsum('nhqk,nkhd->nqhd', attn_probs, values, precision=lax.Precision.HIGHEST)
    attended = low(low_back(attended.reshape(seq_count, seq_length, features)))
    hidden = rows_in + low_back(product(attended, out_matrix))
    normed_mid = low(layer_norm(hidden, norms[2], norms[3]))
    pre_act = low_back(product(normed_mid, up_matrix))
    activated = low(low_back(jax.nn.gelu(pre_act, approximate=True)))
    return hidden + low_back(jnp.einsum('nlf,fd->nld', activated, down_matrix, precision=lax.Precision.HIGHEST))

def image_embed(images_group, frozen, image_norms):
    block_out = block_forward(images_group.astype(jnp.float32), frozen, image_norms, False)
    top_rows = block_out[:, 0]
    return low(top_rows * lax.rsqrt(lax.optimization_barrier(jnp.sum(top_rows * top_rows, axis=-1, keepdims=True)) + EPSILON))

def text_embed(packed, norms, tokens, token_ids):
    block_out = block_forward(tokens, low(packed), norms, True)
    lengths = lax.optimization_barrier(jnp.sum((token_ids != 0).astype(jnp.int32), axis=1))
    pool_mask = (jnp.arange(TXT_LEN, dtype=jnp.int32)[None, :] == (lengths - 1)[:, None]).astype(block_out.dtype)
    pooled = lax.optimization_barrier(jnp.sum(block_out * pool_mask[:, :, None], axis=1))
    return low(pooled * lax.rsqrt(lax.optimization_barrier(jnp.sum(pooled * pooled, axis=-1, keepdims=True)) + EPSILON))

def contrast(text_emb, image_emb, matches, counts):
    logits = LOGIT_SCALE * low_back(product(text_emb, image_emb))
    target = (matches[:, None] == jnp.arange(image_emb.shape[0], dtype=jnp.int32)[None, :]).astype(logits.dtype)
    row_part = jnp.sum(jax.nn.logsumexp(logits, axis=1)) - jnp.sum(logits * target)
    column_part = jnp.sum(jax.nn.logsumexp(logits, axis=0)) - jnp.sum(logits * target / counts.astype(logits.dtype)[None, :])
    return 0.5 * (row_part + column_part)

def reference(images, captions, token_ids, counts, matches, image_weights, image_norms, weights, norm_params, momentum, norm_momentum, averages, norm_averages):
    frozen = image_weights.astype(jnp.float32)
    image_groups = images.reshape(N_DP // 2, 2 * IMG_DEV, IMG_ROWS, D)

    def embed_images(image_group):
        return image_embed(image_group, frozen, image_norms)
    image_emb = lax.map(embed_images, image_groups).reshape(IMAGES, D)
    caption_groups = captions.reshape(N_DP // 2, 2 * CAP_DEV, TXT_LEN, D)
    id_groups = token_ids.reshape(N_DP // 2, 2 * CAP_DEV, TXT_LEN)

    def embed_captions(caption_pair):
        return text_embed(weights, norm_params, caption_pair[0].astype(jnp.float32), caption_pair[1])
    text_emb = lax.map(embed_captions, (caption_groups, id_groups)).reshape(CAPTIONS, D)
    grad_embed = jax.grad(contrast)(text_emb, image_emb, matches, counts).reshape(N_DP // 2, 2 * CAP_DEV, D)

    def one_group(totals, slices):
        tokens, group_ids, cotangent = slices

        def local_embed(packed, norms, rows_in):
            return text_embed(packed, norms, rows_in, group_ids)
        pull = jax.vjp(local_embed, weights, norm_params, tokens.astype(jnp.float32))[1]
        grad_w, grad_n, grad_x = pull(cotangent)
        return ((totals[0] + grad_w, totals[1] + grad_n), grad_x)
    start = (jnp.zeros_like(weights), jnp.zeros_like(norm_params))
    (raw_grads, raw_norm_grads), input_parts = lax.scan(one_group, start, (caption_groups, id_groups, grad_embed))
    input_grad = input_parts.reshape(CAPTIONS, TXT_LEN, D)
    grad_norm = jnp.sqrt(jnp.sum(raw_grads * raw_grads) + jnp.sum(raw_norm_grads * raw_norm_grads))
    factor = jnp.minimum(1.0, CLIP_NORM / (grad_norm + 1e-06))
    grads = raw_grads * factor
    norm_grads = raw_norm_grads * factor
    step_rate = 0.4 * math.sqrt(WROWS)
    decayed = grads + DECAY_RATE * weights
    new_momentum = MOMENTUM_RATE * momentum + decayed
    new_weights = weights - step_rate * (decayed + MOMENTUM_RATE * new_momentum)
    new_averages = AVERAGE_RATE * averages + (1.0 - AVERAGE_RATE) * new_weights
    new_norm_momentum = MOMENTUM_RATE * norm_momentum + norm_grads
    new_norm_params = norm_params - step_rate * (norm_grads + MOMENTUM_RATE * new_norm_momentum)
    new_norm_averages = AVERAGE_RATE * norm_averages + (1.0 - AVERAGE_RATE) * new_norm_params
    return (grads, norm_grads, input_grad, new_weights, new_momentum, new_averages, new_norm_params, new_norm_momentum, new_norm_averages, grad_norm)
```

```python
from functools import partial
import math

import jax
import jax.numpy as jnp
import numpy as np
from jax import lax
from jax.sharding import PartitionSpec as P


HEADS = 12
EPSILON = 1e-06
LOGIT_SCALE = 50.0
CLIP_NORM = 1.0
MOMENTUM_RATE = 0.9
DECAY_RATE = 0.0001
AVERAGE_RATE = 0.7
BOTH = ("tower", "dp")
F32 = jnp.float32
BF16 = jnp.bfloat16


def dot_nt(left, right):
    return lax.dot_general(left, right, (((1,), (1,)), ((), ())), preferred_element_type=F32)


def dot_nn(left, right):
    return lax.dot_general(left, right, (((1,), (0,)), ((), ())), preferred_element_type=F32)


def dot_tn(left, right):
    return lax.dot_general(left, right, (((0,), (0,)), ((), ())), preferred_element_type=F32)


def layer_norm(rows_in, scaling, offset):
    middle = jnp.mean(rows_in, axis=-1, keepdims=True)
    centred = rows_in - middle
    spread = jnp.mean(centred * centred, axis=-1, keepdims=True)
    return centred * lax.rsqrt(spread + EPSILON) * scaling + offset


def swap(block, bit):
    count = lax.axis_size("dp")
    return lax.ppermute(block, "dp", [(i, i ^ bit) for i in range(count)])


def bits_down():
    bit, found = lax.axis_size("dp") // 2, []
    while bit:
        found.append(bit)
        bit //= 2
    return found


def gather_ordered(block):
    place = lax.axis_index("dp")
    held = block[None]
    for bit in bits_down():
        got = swap(held, bit)
        upper = (place // bit) % 2 == 1
        held = jnp.stack([jnp.where(upper, got, held), jnp.where(upper, held, got)], axis=1)
        held = held.reshape((-1,) + block.shape)
    return held


def gather_relative(block):
    held, offsets = block[None], [0]
    for bit in bits_down():
        held = jnp.concatenate([held, swap(held, bit)], axis=0)
        offsets = offsets + [k ^ bit for k in offsets]
    return held, np.array(offsets)


def scatter_relative(held):
    for bit in reversed(bits_down()):
        half = held.shape[0] // 2
        got = swap(held[half:].astype(BF16), bit)
        held = held[:half] + got.astype(F32)
    return held[0]


def scatter_ordered(held):
    place = lax.axis_index("dp")
    for bit in reversed(bits_down()):
        half = held.shape[0] // 2
        pairs = held.reshape((half, 2) + held.shape[1:])
        upper = (place // bit) % 2 == 1
        kept = jnp.where(upper, pairs[:, 1], pairs[:, 0])
        sent = jnp.where(upper, pairs[:, 0], pairs[:, 1])
        held = kept + swap(sent, bit)
    return held[0]


def total(block):
    for bit in bits_down():
        block = block + swap(block, bit)
    return block + lax.ppermute(block, "tower", [(0, 1), (1, 0)])


def colour(moves, devices):
    degree = {}
    for source, _, target, _ in moves:
        degree[("s", source)] = degree.get(("s", source), 0) + 1
        degree[("t", target)] = degree.get(("t", target), 0) + 1
    rounds = max(degree.values())
    at_source = [[None] * rounds for _ in range(devices)]
    at_target = [[None] * rounds for _ in range(devices)]
    for index, (source, _, target, _) in enumerate(moves):
        first = at_source[source].index(None)
        second = at_target[target].index(None)
        if first != second:
            path, wanted, side, node = [], first, "t", target
            while True:
                table = at_target if side == "t" else at_source
                edge = table[node][wanted]
                if edge is None:
                    break
                path.append((edge, wanted))
                node = moves[edge][0] if side == "t" else moves[edge][2]
                side = "s" if side == "t" else "t"
                wanted = second if wanted == first else first
            for edge, old in path:
                at_source[moves[edge][0]][old] = None
                at_target[moves[edge][2]][old] = None
            for edge, old in path:
                new = second if old == first else first
                at_source[moves[edge][0]][new] = edge
                at_target[moves[edge][2]][new] = edge
        at_source[source][first] = index
        at_target[target][first] = index
    return [[at_source[s][r] for s in range(devices)] for r in range(rounds)]


def route(stock, moves, slots, me):
    devices = lax.axis_size("tower") * lax.axis_size("dp")
    arrived = []
    for edges in colour(moves, devices):
        send = np.zeros(devices, np.int32)
        land = np.full(devices, -1, np.int32)
        pairs = []
        for edge in edges:
            if edge is None:
                continue
            source, slot, target, place = moves[edge]
            send[source], land[target] = slot, place
            pairs.append((source, target))
        piece = lax.dynamic_index_in_dim(stock, jnp.asarray(send)[me], 0, keepdims=False)
        arrived.append((lax.ppermute(piece, BOTH, pairs), jnp.asarray(land)[me], set(land.tolist())))
    results = []
    for slot in range(slots):
        value = None
        for piece, place, possible in arrived:
            if slot not in possible:
                continue
            part = jnp.where(place == slot, piece, jnp.zeros_like(piece))
            value = part if value is None else value + part
        results.append(value)
    return results


def head_mask(features):
    feature_head = lax.broadcasted_iota(jnp.int32, (HEADS, 1, features), 2) // (features // HEADS)
    return feature_head == lax.broadcasted_iota(jnp.int32, (HEADS, 1, features), 0)


def spread_heads(rows):
    return jnp.where(head_mask(rows.shape[1]), rows[None], jnp.zeros((), rows.dtype)).reshape(
        HEADS * rows.shape[0], rows.shape[1]
    )


def join_heads(rows, count):
    parts = rows.reshape(HEADS, count, rows.shape[1])
    return jnp.sum(jnp.where(head_mask(rows.shape[1]), parts, 0.0), axis=0)


def pick_rows(position, count, length, padded):
    column = lax.broadcasted_iota(jnp.int32, (padded, count * length), 1)
    row = lax.broadcasted_iota(jnp.int32, (padded, count * length), 0)
    wanted = jnp.pad(position, (0, padded - count))[:, None]
    return (column == row * length + wanted) & (row < count)


def attend(chosen, inside, normed, kv_matrix, qo_matrix, first_rows):
    features = normed.shape[1]
    padded = chosen.shape[0]
    keys = dot_nt(normed, kv_matrix[:features]).astype(BF16)
    values = dot_nt(normed, kv_matrix[features:]).astype(BF16)
    chosen_normed = dot_nn(chosen.astype(BF16), normed).astype(BF16)
    queries = spread_heads(dot_nt(chosen_normed, qo_matrix[:features]).astype(BF16))
    scores = dot_nt(queries, keys) * (features // HEADS) ** (-0.5)
    scores = scores.reshape(HEADS, padded, -1)
    scores = jnp.where(inside[None], scores, -1e30)
    highest = jnp.max(scores, axis=-1, keepdims=True)
    exponent = jnp.exp(scores - highest)
    probs = (exponent / jnp.sum(exponent, axis=-1, keepdims=True)).reshape(HEADS * padded, -1)
    attended = join_heads(dot_nn(probs.astype(BF16), values), padded).astype(BF16)
    hidden = first_rows + dot_nt(attended, qo_matrix[features:])
    return keys, values, chosen_normed, queries, probs, attended, hidden


def local(
    images,
    captions,
    token_ids,
    counts,
    matches,
    image_weights,
    image_norms,
    weights,
    norm_params,
    momentum,
    norm_momentum,
    averages,
    norm_averages,
):
    tower = lax.axis_index("tower")
    place = lax.axis_index("dp")
    spread = lax.axis_size("dp")
    me = tower * spread + place
    is_text = tower == 0
    cap_count, cap_length, features = captions.shape
    img_count, img_length, _ = images.shape
    padded = -(-max(cap_count, img_count) // 8) * 8
    img_padded = -(-(img_count + 1) // 8) * 8
    own_rows = weights.shape[0]
    img_rows = image_weights.shape[0]
    all_rows = own_rows * 2 * spread
    hidden_units = (all_rows - 4 * features) // 2
    unit_rows = hidden_units // spread
    piece = math.gcd(math.gcd(own_rows, img_rows), math.gcd(unit_rows, 2 * features // spread))
    per_own, per_img, per_unit = own_rows // piece, img_rows // piece, unit_rows // piece
    per_matrix = features // piece

    stock = jnp.concatenate([weights.astype(BF16), image_weights], axis=0)
    stock = stock.reshape(-1, piece, features)

    def owner(index):
        return index // per_own, index % per_own

    def attention_home(index):
        matrix, part = index // per_matrix, index % per_matrix
        if matrix in (1, 2):
            return index - per_matrix, 0
        return (part if matrix == 0 else part + per_matrix), 1

    def unit_home(index):
        index = index - 4 * per_matrix
        matrix, part = index // (hidden_units // piece), index % (hidden_units // piece)
        return part // per_unit, matrix * per_unit + part % per_unit

    def incoming(indices, home):
        load = [0] * (2 * spread)
        moves = []
        for index in indices:
            source, slot = owner(index)
            target, where_to = home(index)
            moves.append((source, slot, target, where_to))
            load[source] += 1
        for index in indices:
            near, slot = index // per_img, index % per_img
            source = min((near + spread, near), key=lambda s: load[s])
            target, where_to = home(index)
            moves.append((source, per_own + slot, target + spread, where_to))
            load[source] += 1
        return moves

    attention_pieces = list(range(4 * per_matrix))
    unit_pieces = list(range(4 * per_matrix, all_rows // piece))
    kv_piece, qo_piece = route(stock, incoming(attention_pieces, attention_home), 2, me)
    kv_matrix = gather_ordered(kv_piece).reshape(2 * features, features)
    qo_matrix = gather_ordered(qo_piece).reshape(2 * features, features)
    unit_slots = route(stock, incoming(unit_pieces, unit_home), 2 * per_unit, me)
    up_part = jnp.concatenate(unit_slots[:per_unit], axis=0)
    down_part = jnp.concatenate(unit_slots[per_unit:], axis=0)

    lengths = jnp.sum((token_ids != 0).astype(jnp.int32), axis=1)
    caption_rows = captions.reshape(cap_count * cap_length, features)
    chosen = pick_rows(lengths - 1, cap_count, cap_length, padded)
    column = lax.broadcasted_iota(jnp.int32, (padded, cap_count * cap_length), 1)
    row = lax.broadcasted_iota(jnp.int32, (padded, cap_count * cap_length), 0)
    reach = jnp.pad(lengths, (0, padded - cap_count))[:, None]
    seen = (column >= row * cap_length) & (column < row * cap_length + reach)

    def text_attention(_):
        normed = layer_norm(caption_rows.astype(F32), norm_params[0], norm_params[1]).astype(BF16)
        first_rows = dot_nn(chosen.astype(BF16), caption_rows)
        keys, values, chosen_normed, queries, probs, attended, hidden = attend(
            chosen, seen, normed, kv_matrix, qo_matrix, first_rows
        )
        normed_mid = layer_norm(hidden, norm_params[2], norm_params[3]).astype(BF16)
        return normed, keys, values, chosen_normed, queries, probs, attended, hidden, normed_mid

    def image_attention(_):
        rows = images.reshape(img_count * img_length, features)
        normed = layer_norm(rows.astype(F32), image_norms[0], image_norms[1]).astype(BF16)
        first = jnp.zeros((img_count,), jnp.int32)
        top = pick_rows(first, img_count, img_length, padded)
        column = lax.broadcasted_iota(jnp.int32, (padded, img_count * img_length), 1)
        row = lax.broadcasted_iota(jnp.int32, (padded, img_count * img_length), 0)
        inside = column // img_length == row
        first_rows = dot_nn(top.astype(BF16), rows)
        _, _, _, _, _, _, hidden = attend(top, inside, normed, kv_matrix, qo_matrix, first_rows)
        normed_mid = layer_norm(hidden, image_norms[2], image_norms[3]).astype(BF16)
        flat = jnp.zeros((cap_count * cap_length, features), BF16)
        small = jnp.zeros((padded, features), BF16)
        return (
            flat,
            flat,
            flat,
            small,
            jnp.zeros((HEADS * padded, features), BF16),
            jnp.zeros((HEADS * padded, cap_count * cap_length), F32),
            small,
            hidden,
            normed_mid,
        )

    normed, keys, values, chosen_normed, queries, probs, attended, hidden, normed_mid = lax.cond(
        is_text, text_attention, image_attention, 0
    )
    probs_low = probs.astype(BF16)

    position = lax.broadcasted_iota(jnp.int32, (cap_count * cap_length, cap_length), 0) % cap_length
    fold = (position == lax.broadcasted_iota(jnp.int32, position.shape, 1)).astype(BF16)
    probs_short = dot_nn(probs_low, fold).astype(BF16)
    probs_crossed = lax.ppermute(probs_short, "tower", [(0, 1)])
    attended_crossed = lax.ppermute(attended, "tower", [(0, 1)])

    mid_blocks, offsets = gather_relative(normed_mid)
    mid_rows = mid_blocks.reshape(-1, features)
    pre_act = dot_nt(mid_rows, up_part)
    activated = jax.nn.gelu(pre_act, approximate=True).astype(BF16)
    partial_out = dot_nn(activated, down_part).reshape(mid_blocks.shape)
    block_out = hidden + scatter_relative(partial_out)
    inverse = lax.rsqrt(jnp.sum(block_out * block_out, axis=-1, keepdims=True) + EPSILON)
    emb = (block_out * inverse).astype(BF16)

    img_emb = lax.ppermute(emb[:img_count], "tower", [(1, 0)])
    lane = features // 8
    inverse_row = jnp.pad(inverse[:cap_count, 0], (0, lane - cap_count))
    inverse_high = inverse_row.astype(BF16)
    inverse_mid = (inverse_row - inverse_high.astype(F32)).astype(BF16)
    inverse_low = (
        inverse_row - inverse_high.astype(F32) - inverse_mid.astype(F32)
    ).astype(BF16)
    match_row = jnp.pad(matches, (0, lane - cap_count))
    notes = jnp.concatenate(
        [
            jnp.pad(counts, (0, lane - img_count)).astype(BF16),
            (match_row // 64).astype(BF16),
            (match_row % 64).astype(BF16),
            inverse_high,
            inverse_mid,
            inverse_low,
            jnp.zeros((2 * lane,), BF16),
        ]
    )[None]
    filler = jnp.zeros((img_padded - img_count - 1, features), BF16)
    every, _ = gather_relative(jnp.concatenate([emb, img_emb, notes, filler], axis=0))
    text_all = every[:, :padded].reshape(-1, features)
    img_all = every[:, padded:].reshape(-1, features)
    noted = every[:, padded + img_count].astype(F32).reshape(spread, 8, lane)
    owners = place ^ jnp.asarray(offsets, jnp.int32)
    within = jnp.arange(img_padded, dtype=jnp.int32)[None]
    image_ids = jnp.where(within < img_count, owners[:, None] * img_count + within, -1).reshape(-1)
    image_real = image_ids >= 0
    count_all = jnp.where(within < img_count, noted[:, 0, :img_padded], 1.0).reshape(-1)
    match_all = (noted[:, 1, :padded] * 64.0 + noted[:, 2, :padded]).astype(jnp.int32)
    text_within = jnp.arange(padded, dtype=jnp.int32)[None]
    text_real = jnp.broadcast_to(text_within < cap_count, (spread, padded)).reshape(-1)
    match_all = jnp.where(text_real, match_all.reshape(-1), -2)
    inverse_all = (noted[:, 3] + noted[:, 4] + noted[:, 5])[:, :padded].reshape(-1, 1)

    logits = LOGIT_SCALE * dot_nt(text_all, img_all)
    both_real = text_real[:, None] & image_real[None]
    exponent = jnp.where(both_real, jnp.exp(logits), 0.0)
    row_sum = jnp.sum(exponent, axis=1, keepdims=True)
    column_sum = jnp.sum(exponent, axis=0, keepdims=True)
    target = (match_all[:, None] == image_ids[None]).astype(F32)
    row_scale = 0.5 / jnp.where(text_real[:, None], row_sum, 1.0)
    column_scale = 0.5 / jnp.where(image_real[None], column_sum, 1.0)
    grad_logits = exponent * (row_scale + column_scale) - target * (0.5 + 0.5 / count_all[None])
    scaled_grad = (LOGIT_SCALE * grad_logits).astype(BF16)
    grad_embed = dot_nn(scaled_grad, img_all)
    unit = text_all.astype(F32)
    grad_pooled = inverse_all * (
        grad_embed - jnp.sum(unit * grad_embed, axis=-1, keepdims=True) * unit
    )
    own_embed = grad_embed[:padded]
    own_unit = block_out * inverse
    grad_rows = inverse * (
        own_embed - jnp.sum(own_unit * own_embed, axis=-1, keepdims=True) * own_unit
    )
    own_real = lax.broadcasted_iota(jnp.int32, (padded, 1), 0) < cap_count
    grad_rows = jnp.where(own_real, grad_rows, 0.0)
    grad_branch = jnp.where(text_real[:, None], grad_pooled, 0.0).astype(BF16)

    grad_act = dot_nt(grad_branch, down_part).astype(BF16)
    gelu_pull = jax.vjp(partial(jax.nn.gelu, approximate=True), pre_act)[1]
    grad_pre = gelu_pull(grad_act.astype(F32))[0].astype(BF16)
    grad_mid_rows = scatter_relative(dot_nn(grad_pre, up_part).reshape(mid_blocks.shape))
    grad_up = dot_tn(grad_pre, mid_rows)
    grad_down = dot_tn(activated, grad_branch)
    unit_grads = jnp.concatenate([grad_up, grad_down], axis=0)

    mid_pull = jax.vjp(layer_norm, hidden, norm_params[2], norm_params[3])[1]
    grad_mid_part, grad_gain_mid, grad_shift_mid = mid_pull(grad_mid_rows)
    grad_hidden = jnp.where(own_real, grad_rows + grad_mid_part, 0.0)
    grad_mixed = grad_hidden.astype(BF16)
    grad_att = dot_nn(grad_mixed, qo_matrix[features:]).astype(BF16)
    crossed = lax.ppermute(jnp.concatenate([grad_mixed, grad_att], axis=0), "tower", [(0, 1)])

    def text_attention_back(_):
        gradient = spread_heads(grad_att)
        grad_probs = dot_nt(gradient, values)
        inner = jnp.sum(probs * grad_probs, axis=-1, keepdims=True)
        grad_scores = probs * (grad_probs - inner)
        grad_raw = (grad_scores * (features // HEADS) ** (-0.5)).astype(BF16)
        grad_queries = join_heads(dot_nn(grad_raw, keys), padded).astype(BF16)
        grad_keys = dot_tn(grad_raw, queries).astype(BF16)
        grad_values = dot_tn(probs_low, gradient).astype(BF16)
        shares = jnp.concatenate(
            [dot_tn(grad_keys, normed), dot_tn(grad_queries, chosen_normed)], axis=0
        )
        return shares, grad_keys, grad_values, grad_queries

    def image_attention_back(_):
        text_normed = layer_norm(caption_rows.astype(F32), norm_params[0], norm_params[1])
        wide = jnp.tile(seen, (HEADS, 1))
        probs_wide = jnp.where(wide, dot_nt(probs_crossed, fold), 0.0).astype(BF16)
        gradient = spread_heads(crossed[padded:])
        grad_values = dot_tn(probs_wide, gradient).astype(BF16)
        shares = jnp.concatenate(
            [
                dot_tn(grad_values, text_normed.astype(BF16)),
                dot_tn(crossed[:padded], attended_crossed),
            ],
            axis=0,
        )
        flat = jnp.zeros((cap_count * cap_length, features), BF16)
        return shares, flat, flat, jnp.zeros((padded, features), BF16)

    shares, grad_keys, grad_values, grad_queries = lax.cond(
        is_text, text_attention_back, image_attention_back, 0
    )
    share_piece = scatter_ordered(shares.reshape(spread, piece, features))

    def text_input(_):
        grad_normed = dot_nn(grad_keys, kv_matrix[:features]) + dot_nn(
            grad_values, kv_matrix[features:]
        )
        query_part = dot_nn(grad_queries, qo_matrix[:features])
        pick = jnp.transpose(chosen)
        wide = grad_normed.reshape(cap_count, cap_length, features)
        at_row = (
            lax.broadcasted_iota(jnp.int32, (cap_count, cap_length), 1) == (lengths - 1)[:, None]
        )
        wide = wide + jnp.where(at_row[:, :, None], query_part[:cap_count, None], 0.0)
        pull = jax.vjp(layer_norm, captions.astype(F32), norm_params[0], norm_params[1])[1]
        grad_first, grad_gain, grad_shift = pull(wide)
        result = grad_first + jnp.where(at_row[:, :, None], grad_hidden[:cap_count, None], 0.0)
        half = features // 2
        return (
            result[:, :, :half],
            result[:, :, half:].astype(BF16),
            jnp.stack([grad_gain, grad_shift, grad_gain_mid, grad_shift_mid]),
        )

    def image_input(_):
        blank = jnp.zeros((cap_count, cap_length, features // 2), F32)
        return blank, blank.astype(BF16), jnp.zeros((4, features), F32)

    own_half, given_half, small_grads = lax.cond(is_text, text_input, image_input, 0)
    got_half = lax.ppermute(given_half, "tower", [(0, 1)])
    input_grad = jnp.where(is_text, own_half, got_half.astype(F32))

    squares = jnp.sum(share_piece * share_piece) + jnp.where(
        is_text, jnp.sum(unit_grads * unit_grads), 0.0
    )
    sums = total(jnp.concatenate([small_grads, jnp.full((1, features), squares)], axis=0))
    total_norm_grads = sums[:4]
    grad_norm = jnp.sqrt(sums[4, 0] + jnp.sum(total_norm_grads * total_norm_grads))
    factor = jnp.minimum(1.0, CLIP_NORM / (grad_norm + 1e-06))

    unit_moves = []
    for index in unit_pieces:
        source, slot = unit_home(index)
        target, where_to = owner(index)
        unit_moves.append((source, slot, target, where_to))
    share_moves = []
    for index in attention_pieces:
        matrix, part = index // per_matrix, index % per_matrix
        source = {
            0: part + per_matrix,
            1: part,
            2: part + spread,
            3: part + per_matrix + spread,
        }[matrix]
        target, where_to = owner(index)
        share_moves.append((source, 0, target, where_to))
    unit_owned = route(unit_grads.reshape(-1, piece, features), unit_moves, per_own, me)
    share_owned = route(share_piece[None], share_moves, per_own, me)
    own_grads = jnp.concatenate([a + b for a, b in zip(unit_owned, share_owned)], axis=0)

    grads = own_grads * factor
    norm_grads = total_norm_grads * factor
    step_rate = 0.4 * math.sqrt(all_rows)
    decayed = grads + DECAY_RATE * weights
    new_momentum = MOMENTUM_RATE * momentum + decayed
    new_weights = weights - step_rate * (decayed + MOMENTUM_RATE * new_momentum)
    new_averages = AVERAGE_RATE * averages + (1.0 - AVERAGE_RATE) * new_weights
    new_norm_momentum = MOMENTUM_RATE * norm_momentum + norm_grads
    new_norm_params = norm_params - step_rate * (norm_grads + MOMENTUM_RATE * new_norm_momentum)
    new_norm_averages = AVERAGE_RATE * norm_averages + (1.0 - AVERAGE_RATE) * new_norm_params
    return (
        grads,
        norm_grads,
        input_grad,
        new_weights,
        new_momentum,
        new_averages,
        new_norm_params,
        new_norm_momentum,
        new_norm_averages,
        grad_norm,
    )


def solution(mesh):
    return jax.shard_map(
        local,
        mesh=mesh,
        in_specs=(
            P("dp", None, None),
            P("dp", None, None),
            P("dp", None),
            P("dp"),
            P("dp"),
            P("dp", None),
            P(),
            P(("tower", "dp"), None),
            P(),
            P(("tower", "dp"), None),
            P(),
            P(("tower", "dp"), None),
            P(),
        ),
        out_specs=(
            P(("tower", "dp"), None),
            P(),
            P("dp", None, "tower"),
            P(("tower", "dp"), None),
            P(("tower", "dp"), None),
            P(("tower", "dp"), None),
            P(),
            P(),
            P(),
            P(),
        ),
        check_vma=False,
    )
```
